1024 devices in a mesh: dp: 32 (over y, z_lo), tensor: 32 (over z_hi, x, core).
Axes of the slice: x: 8, y: 8, z: 8 (z_hi: 2, z_lo: 4; z = z_hi * 4 + z_lo), core: 2. Of those that a mesh axis runs over, the one named last changes fastest.
Arguments:
- tokens: bfloat16 [131072, 4096], P(('dp', 'tensor')), may hold values from -24 to 24
- panel: bfloat16 [4096, 1024], P('tensor'), may hold values from -0.09375 to 0.09375
- cotangent: bfloat16 [131072, 512], P(('dp', 'tensor')), may hold values from -6 to 6
Outputs:
- hidden: float32 [131072, 512], P(('dp', 'tensor'))
- grad_panel: float32 [4096, 1024], P('tensor')
The draws below stay inside these ranges and needn't reach their ends.
All inputs are finite; a program needn't handle non-finite values.
Results may differ from the reference program's by a relative error of at most 0.015.
Values may be sent and summed in bfloat16 or wider, within the bound.
No kernel may reach another device: no remote copies, remote signals or barrier semaphores. Data moves between devices by JAX's collectives and lax.ppermute only.
A program may use at most 64 MiB of HBM per device.

```python
import jax
import jax.numpy as jnp
from jax import lax

D = 4096
H = 512
TOK_DEV = 128
TOKENS = 131072
N_DP = 32
N_TENSOR = 32


def raised(entries, own_key, source, target, shards_of, factor):
    owner, partner = [(jnp.arange(entries.shape[position]) // (entries.shape[position] // shards_of)).reshape([-1 if axis == position else 1 for axis in range(entries.ndim)]) for position in (source, target)]
    chosen = jax.random.permutation(own_key, shards_of)[partner]
    strong = (owner == chosen) | (owner == (partner + shards_of // 2) % shards_of)
    return jnp.where(strong, factor * entries, entries)


def block_scale(key, shape, pieces, smallest, largest):
    factor_of = 1.0
    for position, shards_of in pieces:
        heights = jax.random.uniform(jax.random.fold_in(jax.random.fold_in(key, 6), position), (shards_of,), jnp.float32, smallest / len(pieces), largest / len(pieces))
        factor_of = factor_of * jnp.repeat(jnp.exp(heights), shape[position] // shards_of).reshape((-1,) + (1,) * (len(shape) - 1 - position))
    return factor_of


def gaussian(rng, extent, scale, reach, shards=(), held_as=jnp.bfloat16):
    result = jax.random.normal(rng, extent, jnp.float32) * scale
    if len(shards) > 0:
        result = block_scale(rng, extent, shards, -0.22, 0.18) * result
    return jnp.clip(result, min=-reach, max=reach).astype(held_as)


def heavy_noise(key, extent, deviation, reach, pieces, heavy, kind=jnp.bfloat16):
    array = deviation * jax.random.normal(key, extent, jnp.float32)
    if pieces:
        array = array * block_scale(key, extent, pieces, -0.22, 0.18)
    return jnp.clip(raised(array, jax.random.fold_in(key, 3), *heavy), -reach, reach).astype(kind)


def setup_inputs(seed: int = 0) -> dict:
    arg_keys = jax.random.split(jax.random.key(seed), 4)
    return {
        "tokens": heavy_noise(arg_keys[0], (TOKENS, D), 1.0, 24.0, ((0, 1024),), (0, 1, 1024, 6.0)),
        "panel": gaussian(arg_keys[1], (D, 2 * H), D ** -0.5, 0.09375, ((0, 32),)),
        "cotangent": gaussian(arg_keys[2], (TOKENS, H), 1.0, 6.0, ((0, 1024),)),
    }


def reference(tokens, panel, cotangent):
    projected = jnp.dot(tokens, panel, preferred_element_type=jnp.float32)
    gate_pre = projected[:, :H]
    up_pre = projected[:, H:]
    sigmoid_gate = jax.nn.sigmoid(gate_pre)
    hidden = gate_pre * sigmoid_gate * up_pre
    grad_out = cotangent.astype(jnp.float32)
    gate_grad = grad_out * up_pre * sigmoid_gate * (1.0 + gate_pre * (1.0 - sigmoid_gate))
    up_grad = grad_out * gate_pre * sigmoid_gate
    pre_grad = jnp.concatenate([gate_grad, up_grad], axis=1).astype(jnp.bfloat16)
    scale = 1.0 / jnp.sqrt(jnp.float32(TOKENS))
    blocks_tok = tokens.reshape(N_DP * N_TENSOR, TOK_DEV, D)
    blocks_grad = pre_grad.reshape(N_DP * N_TENSOR, TOK_DEV, 2 * H)

    def add_block(running, pair):
        block_tok, block_grad = pair
        grad_term = lax.dot_general(block_tok, block_grad, (((0,), (0,)), ((), ())), preferred_element_type=jnp.float32) * scale
        rounded = lax.optimization_barrier(grad_term.astype(jnp.bfloat16))
        return (running + rounded.astype(jnp.float32), None)
    grad_panel, unused = lax.scan(add_block, jnp.zeros((D, 2 * H), jnp.float32), (blocks_tok, blocks_grad))
    return (hidden, grad_panel)
```

```python
import math

import jax
import jax.numpy as jnp
from jax import lax
from jax.sharding import Mesh, PartitionSpec as P

AXES = ("y", "zlo", "zhi", "x", "core")
NX, NZLO, NZHI, NCORE = 8, 4, 2, 2


def shift(array, step):
    return lax.ppermute(array, "x", [(i, (i + step) % NX) for i in range(NX)])


def swap_cores(array):
    return lax.ppermute(array, "core", [(0, 1), (1, 0)])


def reflect_z(array):
    pairs = [
        (lo * NZHI + hi, (NZLO - 1 - lo) * NZHI + (1 - hi))
        for lo in range(NZLO)
        for hi in range(NZHI)
    ]
    return lax.ppermute(array, ("zlo", "zhi"), pairs)


def on_device(tokens, panel, cotangent):
    rows, width = tokens.shape
    n_dp = lax.axis_size("y") * NZLO
    n_tensor = NZHI * NX * NCORE
    held, panel_cols = panel.shape
    units = panel_cols // 2
    scale = 1.0 / math.sqrt(rows * n_tensor * n_dp)
    x = lax.axis_index("x")
    core = lax.axis_index("core")

    other = reflect_z(panel)
    first = lax.axis_index("zhi") == 0
    own = jnp.concatenate(
        [jnp.where(first, panel, other), jnp.where(first, other, panel)], axis=0
    )
    to_right, to_left = [own], [own]
    for _ in range(3):
        to_right.append(shift(to_right[-1], 1))
        to_left.append(shift(to_left[-1], -1))
    far = (shift(to_right[3][:held], 1), shift(to_left[3][held:], -1))

    def columns(c):
        return jnp.stack(
            [
                jnp.concatenate(
                    [
                        tokens[:, ((z * NX + i) * NCORE + c) * held:][:, :held]
                        for z in range(NZHI)
                    ],
                    axis=1,
                )
                for i in range(NX)
            ]
        )

    by_core = (columns(0), columns(1))
    keep = jnp.where(core == 0, by_core[0], by_core[1])
    give = jnp.where(core == 0, by_core[1], by_core[0])
    pair_tokens = jnp.concatenate([keep, swap_cores(give)], axis=1)

    def toks(step):
        return lax.dynamic_index_in_dim(
            pair_tokens, lax.rem(x + step + NX, NX), 0, keepdims=False
        )

    def dot(a, b):
        return jnp.dot(a, b, preferred_element_type=jnp.float32)

    half = dot(toks(0), own)
    for s in range(1, 4):
        half = half + dot(toks(-s), to_right[s]) + dot(toks(s), to_left[s])
    half = half + dot(toks(4)[:, :held], far[0]) + dot(toks(4)[:, held:], far[1])
    projected = half[:rows] + swap_cores(half[rows:])

    gate_pre = projected[:, :units]
    up_pre = projected[:, units:]
    sigmoid_gate = jax.nn.sigmoid(gate_pre)
    hidden = gate_pre * sigmoid_gate * up_pre
    grad_out = cotangent.astype(jnp.float32)
    gate_grad = grad_out * up_pre * sigmoid_gate * (1.0 + gate_pre * (1.0 - sigmoid_gate))
    up_grad = grad_out * gate_pre * sigmoid_gate
    pre_grad = jnp.concatenate([gate_grad, up_grad], axis=1).astype(jnp.bfloat16)
    pair_grad = jnp.concatenate([pre_grad, swap_cores(pre_grad)], axis=0)

    def term(step):
        product = lax.dot_general(
            toks(step), pair_grad, (((0,), (0,)), ((), ())), preferred_element_type=jnp.float32
        )
        return product * scale

    def wire(value):
        return value.astype(jnp.bfloat16)

    opposite = wire(term(4))
    from_left = shift(opposite[:held], 1).astype(jnp.float32)
    from_right = shift(opposite[held:], -1).astype(jnp.float32)
    for s in (3, 2, 1):
        ahead, behind = term(s), term(-s)
        if s == 3:
            ahead = jnp.concatenate([ahead[:held] + from_left, ahead[held:]], axis=0)
            behind = jnp.concatenate([behind[:held], behind[held:] + from_right], axis=0)
        else:
            ahead, behind = ahead + from_left, behind + from_right
        from_left = shift(wire(ahead), 1).astype(jnp.float32)
        from_right = shift(wire(behind), -1).astype(jnp.float32)
    summed = wire(term(0) + from_left + from_right)

    share = held // n_dp
    pieces = summed.reshape(NZHI, n_dp, share, panel_cols).transpose(1, 0, 2, 3)
    pieces = pieces.reshape(n_dp * NZHI, share, panel_cols)
    met = lax.all_to_all(pieces, ("y", "zlo", "zhi"), 0, 0, tiled=True)
    piece = jnp.sum(met.astype(jnp.float32), axis=0)
    copies = jnp.broadcast_to(piece, (n_dp, share, panel_cols))
    grad_panel = lax.all_to_all(copies, ("y", "zlo"), 0, 0, tiled=True)
    return (hidden, grad_panel.reshape(held, panel_cols))


def solution(mesh):
    fine = Mesh(mesh.devices.reshape(-1, NZLO, NZHI, NX, NCORE), AXES)
    split = P(AXES, None)
    by_tensor = P(("zhi", "x", "core"), None)
    return jax.shard_map(
        on_device,
        mesh=fine,
        in_specs=(split, by_tensor, split),
        out_specs=(split, by_tensor),
        check_vma=False,
    )
```

```python
import math

import jax
import jax.numpy as jnp
from jax import lax
from jax.sharding import Mesh, PartitionSpec as P

AXES = ("y", "zlo", "zhi", "x", "core")
NX, NZLO, NZHI, NCORE = 8, 4, 2, 2


def shift(array, step):
    return lax.ppermute(array, "x", [(i, (i + step) % NX) for i in range(NX)])


def swap_cores(array):
    return lax.ppermute(array, "core", [(0, 1), (1, 0)])


def reflect_z(array):
    pairs = [
        (lo * NZHI + hi, (NZLO - 1 - lo) * NZHI + (1 - hi))
        for lo in range(NZLO)
        for hi in range(NZHI)
    ]
    return lax.ppermute(array, ("zlo", "zhi"), pairs)


def on_device(tokens, panel, cotangent):
    rows, width = tokens.shape
    n_dp = lax.axis_size("y") * NZLO
    n_tensor = NZHI * NX * NCORE
    held, panel_cols = panel.shape
    units = panel_cols // 2
    scale = 1.0 / math.sqrt(rows * n_tensor * n_dp)
    x = lax.axis_index("x")
    core = lax.axis_index("core")

    z_half = lax.axis_index("zhi")
    start = (panel, reflect_z(panel))
    right = [[start[h]] for h in range(NZHI)]
    left = [[start[h]] for h in range(NZHI)]
    for s in range(1, 5):
        for h in range(NZHI):
            if s < 4 or h == 0:
                right[h].append(shift(right[h][-1], 1))
            if s < 4 or h == 1:
                left[h].append(shift(left[h][-1], -1))

    def columns(c):
        return jnp.stack(
            [
                tokens[:, (i * NCORE + c) * held:][:, :held]
                for i in range(NZHI * NX)
            ]
        )

    by_core = (columns(0), columns(1))
    keep = jnp.where(core == 0, by_core[0], by_core[1])
    give = jnp.where(core == 0, by_core[1], by_core[0])
    pair_tokens = jnp.concatenate([keep, swap_cores(give)], axis=1)

    def toks(h, step):
        z = z_half if h == 0 else 1 - z_half
        place = z * NX + lax.rem(x + step + NX, NX)
        return lax.dynamic_index_in_dim(pair_tokens, place, 0, keepdims=False)

    def dot(a, b):
        return jnp.dot(a, b, preferred_element_type=jnp.float32)

    half = dot(toks(0, 0), start[0])
    for s in range(1, 5):
        for h in range(NZHI):
            if s == 1 and h == 1:
                half = half + dot(toks(1, 0), start[1])
            if s < 4 or h == 0:
                half = half + dot(toks(h, -s), right[h][s])
            if s < 4 or h == 1:
                half = half + dot(toks(h, s), left[h][s])
    projected = half[:rows] + swap_cores(half[rows:])

    gate_pre = projected[:, :units]
    up_pre = projected[:, units:]
    sigmoid_gate = jax.nn.sigmoid(gate_pre)
    hidden = gate_pre * sigmoid_gate * up_pre
    grad_out = cotangent.astype(jnp.float32)
    gate_grad = grad_out * up_pre * sigmoid_gate * (1.0 + gate_pre * (1.0 - sigmoid_gate))
    up_grad = grad_out * gate_pre * sigmoid_gate
    pre_grad = jnp.concatenate([gate_grad, up_grad], axis=1).astype(jnp.bfloat16)
    pair_grad = jnp.concatenate([pre_grad, swap_cores(pre_grad)], axis=0)

    def term(h, step):
        product = lax.dot_general(
            toks(h, step), pair_grad, (((0,), (0,)), ((), ())),
            preferred_element_type=jnp.float32,
        )
        return product * scale

    def wire(value):
        return value.astype(jnp.bfloat16)

    going_right, going_left = [None, None], [None, None]
    for s in (4, 3, 2, 1):
        for h in range(NZHI):
            if s < 4 or h == 0:
                ahead = term(h, s)
                if going_right[h] is not None:
                    ahead = ahead + going_right[h].astype(jnp.float32)
                going_right[h] = shift(wire(ahead), 1)
            if s < 4 or h == 1:
                behind = term(h, -s)
                if going_left[h] is not None:
                    behind = behind + going_left[h].astype(jnp.float32)
                going_left[h] = shift(wire(behind), -1)
    sums = [
        wire(
            term(h, 0)
            + going_right[h].astype(jnp.float32)
            + going_left[h].astype(jnp.float32)
        )
        for h in range(NZHI)
    ]
    summed = jnp.where(z_half == 0, jnp.stack(sums), jnp.stack(sums[::-1]))

    share = held // n_dp
    pieces = summed.reshape(NZHI, n_dp, share, panel_cols).transpose(1, 0, 2, 3)
    pieces = pieces.reshape(n_dp * NZHI, share, panel_cols)
    met = lax.all_to_all(pieces, ("y", "zlo", "zhi"), 0, 0, tiled=True)
    piece = jnp.sum(met.astype(jnp.float32), axis=0)
    copies = jnp.broadcast_to(piece, (n_dp, share, panel_cols))
    grad_panel = lax.all_to_all(copies, ("y", "zlo"), 0, 0, tiled=True)
    return (hidden, grad_panel.reshape(held, panel_cols))


def solution(mesh):
    fine = Mesh(mesh.devices.reshape(-1, NZLO, NZHI, NX, NCORE), AXES)
    split = P(AXES, None)
    by_tensor = P(("zhi", "x", "core"), None)
    return jax.shard_map(
        on_device,
        mesh=fine,
        in_specs=(split, by_tensor, split),
        out_specs=(split, by_tensor),
        check_vma=False,
    )
```

```python
import math

import jax
import jax.numpy as jnp
from jax import lax
from jax.sharding import Mesh, PartitionSpec as P

AXES = ("y", "zlo", "zhi", "x", "core")
NX, NZLO, NZHI, NCORE = 8, 4, 2, 2


def shift(array, step):
    pairs = [
        (i * NCORE + c, (i + (step if c == 0 else -step)) % NX * NCORE + c)
        for i in range(NX)
        for c in range(NCORE)
    ]
    return lax.ppermute(array, ("x", "core"), pairs)


def swap_cores(array):
    return lax.ppermute(array, "core", [(0, 1), (1, 0)])


def reflect_z(array):
    pairs = [
        (lo * NZHI + hi, (NZLO - 1 - lo) * NZHI + (1 - hi))
        for lo in range(NZLO)
        for hi in range(NZHI)
    ]
    return lax.ppermute(array, ("zlo", "zhi"), pairs)


def on_device(tokens, panel, cotangent):
    rows, width = tokens.shape
    n_dp = lax.axis_size("y") * NZLO
    n_tensor = NZHI * NX * NCORE
    held, panel_cols = panel.shape
    units = panel_cols // 2
    scale = 1.0 / math.sqrt(rows * n_tensor * n_dp)
    x = lax.axis_index("x")
    core = lax.axis_index("core")

    z_half = lax.axis_index("zhi")
    start = (panel, reflect_z(panel))
    right = [[start[h]] for h in range(NZHI)]
    left = [[start[h]] for h in range(NZHI)]
    for s in range(1, 5):
        for h in range(NZHI):
            if s < 4 or h == 0:
                right[h].append(shift(right[h][-1], 1))
            if s < 4 or h == 1:
                left[h].append(shift(left[h][-1], -1))

    tokens, _ = lax.optimization_barrier((tokens, start[1]))

    def columns(c):
        return jnp.stack(
            [
                jnp.concatenate(
                    [
                        tokens[:, ((z * NX + i) * NCORE + c) * held:][:, :held]
                        for z in range(NZHI)
                    ],
                    axis=1,
                )
                for i in range(NX)
            ]
        )

    by_core = (columns(0), columns(1))
    keep = jnp.where(core == 0, by_core[0], by_core[1])
    give = jnp.where(core == 0, by_core[1], by_core[0])
    pair_tokens = jnp.concatenate([keep, swap_cores(give)], axis=1)
    by_z = (pair_tokens[:, :, :held], pair_tokens[:, :, held:])
    by_half = (
        jnp.where(z_half == 0, by_z[0], by_z[1]),
        jnp.where(z_half == 0, by_z[1], by_z[0]),
    )
    sense = 1 - 2 * core

    def toks(h, step):
        place = lax.rem(x + sense * step + NX, NX)
        return lax.dynamic_index_in_dim(by_half[h], place, 0, keepdims=False)

    def dot(a, b):
        return jnp.dot(a, b, preferred_element_type=jnp.float32)

    half = dot(toks(0, 0), start[0])
    for s in range(1, 5):
        for h in range(NZHI):
            if s == 1 and h == 1:
                half = half + dot(toks(1, 0), start[1])
            if s < 4 or h == 0:
                half = half + dot(toks(h, -s), right[h][s])
            if s < 4 or h == 1:
                half = half + dot(toks(h, s), left[h][s])
    projected = half[:rows] + swap_cores(half[rows:])

    gate_pre = projected[:, :units]
    up_pre = projected[:, units:]
    sigmoid_gate = jax.nn.sigmoid(gate_pre)
    hidden = gate_pre * sigmoid_gate * up_pre
    grad_out = cotangent.astype(jnp.float32)
    gate_grad = grad_out * up_pre * sigmoid_gate * (1.0 + gate_pre * (1.0 - sigmoid_gate))
    up_grad = grad_out * gate_pre * sigmoid_gate
    pre_grad = jnp.concatenate([gate_grad, up_grad], axis=1).astype(jnp.bfloat16)
    pair_grad = jnp.concatenate([pre_grad, swap_cores(pre_grad)], axis=0)

    def term(h, step):
        product = lax.dot_general(
            toks(h, step), pair_grad, (((0,), (0,)), ((), ())),
            preferred_element_type=jnp.float32,
        )
        return product * scale

    def wire(value):
        return value.astype(jnp.bfloat16)

    going_right, going_left = [None, None], [None, None]
    for s in (4, 3, 2, 1):
        for h in range(NZHI):
            if s < 4 or h == 0:
                ahead = term(h, s)
                if going_right[h] is not None:
                    ahead = ahead + going_right[h].astype(jnp.float32)
                going_right[h] = shift(wire(ahead), 1)
            if s < 4 or h == 1:
                behind = term(h, -s)
                if going_left[h] is not None:
                    behind = behind + going_left[h].astype(jnp.float32)
                going_left[h] = shift(wire(behind), -1)
    sums = [
        wire(
            term(h, 0)
            + going_right[h].astype(jnp.float32)
            + going_left[h].astype(jnp.float32)
        )
        for h in range(NZHI)
    ]
    summed = jnp.where(z_half == 0, jnp.stack(sums), jnp.stack(sums[::-1]))

    share = held // n_dp
    pieces = summed.reshape(NZHI, n_dp, share, panel_cols).transpose(1, 0, 2, 3)
    pieces = pieces.reshape(n_dp * NZHI, share, panel_cols)
    met = lax.all_to_all(pieces, ("y", "zlo", "zhi"), 0, 0, tiled=True)
    piece = jnp.sum(met.astype(jnp.float32), axis=0)
    copies = jnp.broadcast_to(piece, (n_dp, share, panel_cols))
    grad_panel = lax.all_to_all(copies, ("y", "zlo"), 0, 0, tiled=True)
    return (hidden, grad_panel.reshape(held, panel_cols))


def solution(mesh):
    fine = Mesh(mesh.devices.reshape(-1, NZLO, NZHI, NX, NCORE), AXES)
    split = P(AXES, None)
    by_tensor = P(("zhi", "x", "core"), None)
    return jax.shard_map(
        on_device,
        mesh=fine,
        in_specs=(split, by_tensor, split),
        out_specs=(split, by_tensor),
        check_vma=False,
    )
```

```python
import math

import jax
import jax.numpy as jnp
from jax import lax
from jax.sharding import Mesh, PartitionSpec as P


AXES = ("y", "zlo", "zhi", "x", "core")
NX, NZLO, NZHI, NCORE = 8, 4, 2, 2


def shift(array, step):
    return lax.ppermute(array, "x", [(i, (i + step) % NX) for i in range(NX)])


def swap_cores(array):
    return lax.ppermute(array, "core", [(0, 1), (1, 0)])


def reflect_z(array):
    pairs = [
        (lo * NZHI + hi, (NZLO - 1 - lo) * NZHI + (1 - hi))
        for lo in range(NZLO)
        for hi in range(NZHI)
    ]
    return lax.ppermute(array, ("zlo", "zhi"), pairs)


def compute(tokens, panel, cotangent):
    rows, _ = tokens.shape
    n_dp = lax.axis_size("y") * NZLO
    n_tensor = NZHI * NX * NCORE
    held, panel_cols = panel.shape
    units = panel_cols // 2
    scale = 1.0 / math.sqrt(rows * n_tensor * n_dp)
    x = lax.axis_index("x")
    core = lax.axis_index("core")

    z_half = lax.axis_index("zhi")
    start = (panel, reflect_z(panel))
    right = [[start[h]] for h in range(NZHI)]
    left = [[start[h]] for h in range(NZHI)]
    right[0].append(shift(start[0], 1))
    left[0].append(shift(start[0], -1))
    for s in range(1, 5):
        if s < 4:
            right[1].append(shift(right[1][-1], 1))
            right[0].append(shift(right[0][-1], 1))
        if s < 3:
            left[0].append(shift(left[0][-1], -1))
        left[1].append(shift(left[1][-1], -1))

    tokens, _ = lax.optimization_barrier((tokens, start[1]))

    def columns(c):
        return jnp.stack(
            [
                jnp.concatenate(
                    [
                        tokens[:, ((z * NX + i) * NCORE + c) * held:][:, :held]
                        for z in range(NZHI)
                    ],
                    axis=1,
                )
                for i in range(NX)
            ]
        )

    by_core = (columns(0), columns(1))
    keep = jnp.where(core == 0, by_core[0], by_core[1])
    give = jnp.where(core == 0, by_core[1], by_core[0])
    pair_tokens = jnp.concatenate([keep, swap_cores(give)], axis=1)
    by_z = (pair_tokens[:, :, :held], pair_tokens[:, :, held:])
    by_half = (
        jnp.where(z_half == 0, by_z[0], by_z[1]),
        jnp.where(z_half == 0, by_z[1], by_z[0]),
    )

    def toks(h, step):
        place = lax.rem(x + step + NX, NX)
        return lax.dynamic_index_in_dim(by_half[h], place, 0, keepdims=False)

    def dot(a, b):
        return jnp.dot(a, b, preferred_element_type=jnp.float32)

    half = dot(toks(0, 0), start[0])
    for s in range(1, 5):
        for h in range(NZHI):
            if s == 1 and h == 1:
                half = half + dot(toks(1, 0), start[1])
            if s < 4 or h == 0:
                half = half + dot(toks(h, -s), right[h][s])
            if s < 4 or h == 1:
                half = half + dot(toks(h, s), left[h][s])
    projected = half[:rows] + swap_cores(half[rows:])

    gate_pre = projected[:, :units]
    up_pre = projected[:, units:]
    sigmoid_gate = jax.nn.sigmoid(gate_pre)
    hidden = gate_pre * sigmoid_gate * up_pre
    grad_out = cotangent.astype(jnp.float32)
    gate_grad = grad_out * up_pre * sigmoid_gate * (1.0 + gate_pre * (1.0 - sigmoid_gate))
    up_grad = grad_out * gate_pre * sigmoid_gate
    pre_grad = jnp.concatenate([gate_grad, up_grad], axis=1).astype(jnp.bfloat16)
    pair_grad = jnp.concatenate([pre_grad, swap_cores(pre_grad)], axis=0)

    def term(h, step):
        product = lax.dot_general(
            toks(h, step), pair_grad, (((0,), (0,)), ((), ())),
            preferred_element_type=jnp.float32,
        )
        return product * scale

    def wire(value):
        return value.astype(jnp.bfloat16)

    going_right, going_left = [None, None], [None, None]
    for s in (4, 3, 2, 1):
        for h, step in ((0, s), (1, s - 1)):
            if step > 0:
                ahead = term(h, step)
                if going_right[h] is not None:
                    ahead = ahead + going_right[h].astype(jnp.float32)
                going_right[h] = shift(wire(ahead), 1)
        for h, step in ((1, s), (0, s - 1)):
            if step > 0:
                behind = term(h, -step)
                if going_left[h] is not None:
                    behind = behind + going_left[h].astype(jnp.float32)
                going_left[h] = shift(wire(behind), -1)
    sums = [
        wire(
            term(h, 0)
            + going_right[h].astype(jnp.float32)
            + going_left[h].astype(jnp.float32)
        )
        for h in range(NZHI)
    ]
    summed = jnp.where(z_half == 0, jnp.stack(sums), jnp.stack(sums[::-1]))

    share = held // n_dp
    pieces = summed.reshape(NZHI, n_dp, share, panel_cols).transpose(1, 0, 2, 3)
    pieces = pieces.reshape(n_dp * NZHI, share, panel_cols)
    met = lax.all_to_all(pieces, ("y", "zlo", "zhi"), 0, 0, tiled=True)
    piece = jnp.sum(met.astype(jnp.float32), axis=0)
    copies = jnp.broadcast_to(piece, (n_dp, share, panel_cols))
    grad_panel = lax.all_to_all(copies, ("y", "zlo"), 0, 0, tiled=True)
    return (hidden, grad_panel.reshape(held, panel_cols))


def solution(mesh):
    fine = Mesh(mesh.devices.reshape(-1, NZLO, NZHI, NX, NCORE), AXES)
    split = P(AXES, None)
    by_tensor = P(("zhi", "x", "core"), None)
    return jax.shard_map(
        compute,
        mesh=fine,
        in_specs=(split, by_tensor, split),
        out_specs=(split, by_tensor),
        check_vma=False,
    )
```

```python
import math

import jax
import jax.numpy as jnp
from jax import lax
from jax.sharding import Mesh, PartitionSpec as P

AXES = ("y", "zlo", "zhi", "x", "core")
NX, NZLO, NZHI, NCORE = 8, 4, 2, 2


def shift(array, step):
    return lax.ppermute(array, "x", [(i, (i + step) % NX) for i in range(NX)])


def swap_cores(array):
    return lax.ppermute(array, "core", [(0, 1), (1, 0)])


def reflect_z(array):
    pairs = [
        (lo * NZHI + hi, (NZLO - 1 - lo) * NZHI + (1 - hi))
        for lo in range(NZLO)
        for hi in range(NZHI)
    ]
    return lax.ppermute(array, ("zlo", "zhi"), pairs)


def on_device(tokens, panel, cotangent):
    rows, width = tokens.shape
    n_dp = lax.axis_size("y") * NZLO
    n_tensor = NZHI * NX * NCORE
    held, panel_cols = panel.shape
    units = panel_cols // 2
    scale = 1.0 / math.sqrt(rows * n_tensor * n_dp)
    x = lax.axis_index("x")
    core = lax.axis_index("core")

    z_half = lax.axis_index("zhi")
    start = (panel, reflect_z(panel))
    right = [[start[h]] for h in range(NZHI)]
    left = [[start[h]] for h in range(NZHI)]
    right[0].append(shift(start[0], 1))
    left[0].append(shift(start[0], -1))
    for s in range(1, 5):
        if s < 4:
            right[1].append(shift(right[1][-1], 1))
            right[0].append(shift(right[0][-1], 1))
        if s < 3:
            left[0].append(shift(left[0][-1], -1))
        left[1].append(shift(left[1][-1], -1))

    tokens, _ = lax.optimization_barrier((tokens, right[0][1]))

    def columns(c):
        return jnp.stack(
            [
                jnp.concatenate(
                    [
                        tokens[:, ((z * NX + i) * NCORE + c) * held:][:, :held]
                        for z in range(NZHI)
                    ],
                    axis=1,
                )
                for i in range(NX)
            ]
        )

    by_core = (columns(0), columns(1))
    keep = jnp.where(core == 0, by_core[0], by_core[1])
    give = jnp.where(core == 0, by_core[1], by_core[0])
    pair_tokens = jnp.concatenate([keep, swap_cores(give)], axis=1)
    by_z = (pair_tokens[:, :, :held], pair_tokens[:, :, held:])
    by_half = (
        jnp.where(z_half == 0, by_z[0], by_z[1]),
        jnp.where(z_half == 0, by_z[1], by_z[0]),
    )

    def toks(h, step):
        place = lax.rem(x + step + NX, NX)
        return lax.dynamic_index_in_dim(by_half[h], place, 0, keepdims=False)

    def dot(a, b):
        return jnp.dot(a, b, preferred_element_type=jnp.float32)

    half = dot(toks(0, 0), start[0])
    for s in range(1, 5):
        for h in range(NZHI):
            if s == 1 and h == 1:
                half = half + dot(toks(1, 0), start[1])
            if s < 4 or h == 0:
                half = half + dot(toks(h, -s), right[h][s])
            if s < 4 or h == 1:
                half = half + dot(toks(h, s), left[h][s])
    projected = half[:rows] + swap_cores(half[rows:])

    gate_pre = projected[:, :units]
    up_pre = projected[:, units:]
    sigmoid_gate = jax.nn.sigmoid(gate_pre)
    hidden = gate_pre * sigmoid_gate * up_pre
    grad_out = cotangent.astype(jnp.float32)
    gate_grad = grad_out * up_pre * sigmoid_gate * (1.0 + gate_pre * (1.0 - sigmoid_gate))
    up_grad = grad_out * gate_pre * sigmoid_gate
    pre_grad = jnp.concatenate([gate_grad, up_grad], axis=1).astype(jnp.bfloat16)
    pair_grad = jnp.concatenate([pre_grad, swap_cores(pre_grad)], axis=0)

    def term(h, step):
        product = lax.dot_general(
            toks(h, step), pair_grad, (((0,), (0,)), ((), ())),
            preferred_element_type=jnp.float32,
        )
        return product * scale

    def wire(value):
        return value.astype(jnp.bfloat16)

    going_right, going_left = [None, None], [None, None]
    for s in (4, 3, 2, 1):
        for h, step in ((0, s), (1, s - 1)):
            if step > 0:
                ahead = term(h, step)
                if going_right[h] is not None:
                    ahead = ahead + going_right[h].astype(jnp.float32)
                going_right[h] = shift(wire(ahead), 1)
        for h, step in ((1, s), (0, s - 1)):
            if step > 0:
                behind = term(h, -step)
                if going_left[h] is not None:
                    behind = behind + going_left[h].astype(jnp.float32)
                going_left[h] = shift(wire(behind), -1)
    sums = [
        wire(
            term(h, 0)
            + going_right[h].astype(jnp.float32)
            + going_left[h].astype(jnp.float32)
        )
        for h in range(NZHI)
    ]
    summed = jnp.where(z_half == 0, jnp.stack(sums), jnp.stack(sums[::-1]))

    share = held // n_dp
    pieces = summed.reshape(NZHI, n_dp, share, panel_cols).transpose(1, 0, 2, 3)
    pieces = pieces.reshape(n_dp * NZHI, share, panel_cols)
    met = lax.all_to_all(pieces, ("y", "zlo", "zhi"), 0, 0, tiled=True)
    piece = jnp.sum(met.astype(jnp.float32), axis=0)
    copies = jnp.broadcast_to(piece, (n_dp, share, panel_cols))
    grad_panel = lax.all_to_all(copies, ("y", "zlo"), 0, 0, tiled=True)
    return (hidden, grad_panel.reshape(held, panel_cols))


def solution(mesh):
    fine = Mesh(mesh.devices.reshape(-1, NZLO, NZHI, NX, NCORE), AXES)
    split = P(AXES, None)
    by_tensor = P(("zhi", "x", "core"), None)
    return jax.shard_map(
        on_device,
        mesh=fine,
        in_specs=(split, by_tensor, split),
        out_specs=(split, by_tensor),
        check_vma=False,
    )
```
